32 devices in a mesh: rep: 8 (over y, x, core), shard: 4 (over z).
Axes of the slice: x: 2, y: 2, z: 4, core: 2. Of those that a mesh axis runs over, the one named last changes fastest.
Arguments:
- tokens: bfloat16 [8, 1024, 768], P('rep', 'shard'), may hold values from -6 to 6
- cotangent: bfloat16 [8, 1024, 768], P('rep', 'shard'), may hold values from -6 to 6
- lengths: int32 [8, 4], P('rep'), may hold values from 1 to 512, 1024 in all within a row
- deal: int32 [8, 1024], P('rep'), may hold values from 0 to 1023, each once within a row
- attn_master: float32 [4, 768, 768], P(None, 'shard'), may hold values from -3 to 3
- ffin_master: float32 [2, 768, 2048], P(None, 'shard'), may hold values from -0.21875 to 0.21875
- ffout_master: float32 [2048, 768], P('shard'), may hold values from -0.125 to 0.125
- gain_master: float32 [2, 768], P(None, 'shard'), may hold values from 0.5 to 1.5
- bias_master: float32 [32, 12], P('shard'), may hold values from -4 to 4
- attn_first: float32 [4, 768, 768], P(None, 'shard'), may hold values from -286.72 to 286.72
- ffin_first: float32 [2, 768, 2048], P(None, 'shard'), may hold values from -30.320738 to 30.320738
- ffout_first: float32 [2048, 768], P('shard'), may hold values from -32.58348 to 32.58348
- gain_first: float32 [2, 768], P(None, 'shard'), may hold values from -75.57557 to 75.57557
- bias_first: float32 [32, 12], P('shard'), may hold values from -284.16 to 284.16
- attn_second: float32 [4, 768, 768], P(None, 'shard'), may hold values from 32.768 to 112721.92
- ffin_second: float32 [2, 768, 2048], P(None, 'shard'), may hold values from 155.648 to 1245.184
- ffout_second: float32 [2048, 768], P('shard'), may hold values from 181.8624 to 1458.176
- gain_second: float32 [2, 768], P(None, 'shard'), may hold values from 966.656 to 7782.4
- bias_second: float32 [32, 12], P('shard'), may hold values from 2097.152 to 16777.217
Outputs:
- layer_out: bfloat16 [8, 1024, 768], P('rep', 'shard')
- input_grad: bfloat16 [8, 1024, 768], P('rep', 'shard')
- attn_new: float32 [4, 768, 768], P(None, 'shard')
- ffin_new: float32 [2, 768, 2048], P(None, 'shard')
- ffout_new: float32 [2048, 768], P('shard')
- gain_step: float32 [2, 768], P(None, 'shard')
- bias_step: float32 [32, 12], P('shard')
- attn_first_new: float32 [4, 768, 768], P(None, 'shard')
- ffin_first_new: float32 [2, 768, 2048], P(None, 'shard')
- ffout_first_new: float32 [2048, 768], P('shard')
- gain_first_new: float32 [2, 768], P(None, 'shard')
- bias_first_new: float32 [32, 12], P('shard')
- attn_second_new: float32 [3, 768, 768], P(None, 'shard')
- wo_second_new: float32 [768, 768], P('shard')
- ffin_second_new: float32 [2, 768, 2048], P(None, 'shard')
- ffout_second_new: float32 [2048, 768], P('shard')
- gain_second_new: float32 [2, 768], P(None, 'shard')
- bias_second_new: float32 [32, 12], P('shard')
- attn_copy: bfloat16 [4, 768, 768], P(None, 'shard')
- ffin_copy: bfloat16 [2, 768, 2048], P(None, 'shard')
- ffout_copy: bfloat16 [2048, 768], P('shard')
The draws below stay inside these ranges and needn't reach their ends.
Inputs may be any that keep to these rules, and one draw needn't show every extreme that they name: Each row holds the 4 lengths of one group's packed sequences; they sum to 1024 and the longest is exactly 512. `deal`: each row is a permutation of 0 to 1023.
All inputs are finite; a program needn't handle non-finite values.
Results may differ from the reference program's by a relative error of at most 0.03.
Values may be sent and summed in bfloat16 or wider, within the bound.
No kernel may reach another device: no remote copies, remote signals or barrier semaphores. Data moves between devices by JAX's collectives and lax.ppermute only.
A program may use at most 192 MiB of HBM per device.

```python
import math
import jax
import jax.numpy as jnp
import numpy as np
from jax import lax

D = 768
H = 12
HD = 64
FF = 2048
NB = 32
NSEQ = 4
TOKG = 1024
LONGEST = 512
N_REP = 8


def draw_attn_master(key, part):
    spread = jnp.array([(D * HD) ** (-0.5), D ** (-0.5), D ** (-0.5), (TOKG / (32.0 * D)) ** 0.5], jnp.float32)
    values = jnp.clip(jax.random.normal(key, (4, D, D), jnp.float32), -5.0, 5.0)
    return values * spread[:, None, None]


def grad_sizes():
    whole = (N_REP * TOKG) ** 0.5
    return jnp.array([(TOKG / 32.0) ** 0.5, 1.5, 1.5, 0.3], jnp.float32) * whole


def draw_attn_first(key, part):
    values = jnp.clip(jax.random.normal(key, (4, D, D), jnp.float32), -5.0, 5.0)
    return values * (0.111 * grad_sizes())[:, None, None]


def draw_attn_second(key, part):
    factor = jnp.exp(jax.random.uniform(key, (4, D, D), jnp.float32, 0.0, 2.0794))
    sizes = grad_sizes()
    return factor * (0.0526 * sizes * sizes)[:, None, None]


def level_of(rng, shape, cuts, low, top_value):
    def one(axis_at, shards_of):
        draws = jax.random.uniform(jax.random.fold_in(jax.random.fold_in(rng, 6), axis_at), (shards_of,), jnp.float32, low / len(cuts), top_value / len(cuts))
        return jnp.repeat(jnp.exp(draws), shape[axis_at] // shards_of).reshape((-1,) + (1,) * (len(shape) - axis_at - 1))

    factor_of = one(*cuts[0])
    for cut in cuts[1:]:
        factor_of = factor_of * one(*cut)
    return factor_of


def profile(amount, total, most, skew):
    weights = [(1 << 20) // math.isqrt(standing ** skew) + 1 for standing in range(2, amount + 1)]
    spare, holding = total - most - (amount - 1), [1] * (amount - 1)
    while spare > 0:
        movable = [i for i in range(amount - 1) if holding[i] < most]
        whole, left = sum([weights[i] for i in movable]), spare
        for i in movable:
            more = min(most - holding[i], max(1, left * weights[i] // whole), spare)
            holding[i] = holding[i] + more
            spare = spare - more
    return np.array([most] + holding)


def ragged(own_key, number_of, total, most, slope):
    if number_of == 2:
        one = jax.random.randint(own_key, (), max(1, total - most), min(most, total - 1) + 1)
        return jnp.stack([one, total - one])
    tallies = jnp.asarray(profile(number_of, total, most, slope), jnp.int32)
    twos = (number_of - 1) // 2
    donor, taker = tallies[1:1 + 2 * twos:2], tallies[2:2 + 2 * twos:2]
    room = jnp.minimum(donor - 1, most - taker)
    moved = jax.random.randint(jax.random.fold_in(own_key, 1), (twos,), 0, 1 << 20) % (room + 1)
    tallies = tallies.at[1:1 + 2 * twos:2].set(donor - moved).at[2:2 + 2 * twos:2].set(taker + moved)
    return tallies[jax.random.permutation(jax.random.fold_in(own_key, 2), number_of)]


def bell_draw(key, extent, scale, bound, shards=(), kind=jnp.bfloat16):
    drawn = scale * jax.random.normal(key, extent, jnp.float32)
    if shards:
        drawn = drawn * level_of(key, extent, shards, -0.22, 0.18)
    return jnp.clip(drawn, -bound, bound).astype(kind)


def setup_inputs(seed: int = 0) -> dict:
    streams_of = jax.random.split(jax.random.key(seed), 20)
    tokens = bell_draw(streams_of[0], (N_REP, TOKG, D), 1.0, 6.0, ((0, 8), (1, 4)))
    cotangent = bell_draw(streams_of[1], (N_REP, TOKG, D), 1.0, 6.0, ((0, 8), (1, 4)))
    lengths = jax.vmap(lambda own: ragged(own, NSEQ, TOKG, LONGEST, 0))(jax.random.split(streams_of[2], N_REP)).reshape((N_REP, NSEQ)).astype(jnp.int32)
    deal = jax.vmap(lambda own: jax.random.permutation(own, TOKG))(jax.random.split(streams_of[3], N_REP)).reshape((N_REP, TOKG)).astype(jnp.int32)
    attn_master = draw_attn_master(jax.random.fold_in(streams_of[19], 71), 0)
    ffin_master = bell_draw(streams_of[5], (2, D, FF), D ** -0.5, 0.21875, ((1, 4),), jnp.float32)
    ffout_master = bell_draw(streams_of[6], (FF, D), FF ** -0.5, 0.125, ((0, 4),), jnp.float32)
    gain_master = jnp.clip(1.0 + 0.1 * jax.random.normal(streams_of[7], (2, D), jnp.float32), 0.5, 1.5)
    bias_master = bell_draw(streams_of[8], (NB, H), 1.0, 4.0, ((0, 4),), jnp.float32)
    attn_first = draw_attn_first(jax.random.fold_in(streams_of[19], 71), 0)
    ffin_first = bell_draw(streams_of[10], (2, D, FF), (0.067 * (N_REP * TOKG) ** 0.5), 30.320738, ((1, 4),), jnp.float32)
    ffout_first = bell_draw(streams_of[11], (FF, D), (0.072 * (N_REP * TOKG) ** 0.5), 32.58348, ((0, 4),), jnp.float32)
    gain_first = bell_draw(streams_of[12], (2, D), (0.167 * (N_REP * TOKG) ** 0.5), 75.57557, ((1, 4),), jnp.float32)
    bias_first = bell_draw(streams_of[13], (NB, H), (0.111 * (N_REP * TOKG * TOKG / 32) ** 0.5), 284.16, ((0, 4),), jnp.float32)
    attn_second = draw_attn_second(jax.random.fold_in(streams_of[19], 71), 0)
    ffin_second = jnp.clip(jnp.exp(math.log(1245.184) - 2.0794415 * jax.random.uniform(streams_of[15], (2, D, FF), jnp.float32) ** level_of(streams_of[15], (2, D, FF), ((1, 4),), -0.2, 0.2)), 155.648, 1245.184)
    ffout_second = jnp.clip(jnp.exp(math.log(1458.176) - 2.0816913 * jax.random.uniform(streams_of[16], (FF, D), jnp.float32) ** level_of(streams_of[16], (FF, D), ((0, 4),), -0.2, 0.2)), 181.8624, 1458.176)
    gain_second = jnp.clip(jnp.exp(math.log(7782.4) - 2.0857773 * jax.random.uniform(streams_of[17], (2, D), jnp.float32) ** level_of(streams_of[17], (2, D), ((1, 4),), -0.2, 0.2)), 966.656, 7782.4)
    bias_second = jnp.clip(jnp.exp(math.log(16777.217) - 2.0794415 * jax.random.uniform(streams_of[18], (NB, H), jnp.float32) ** level_of(streams_of[18], (NB, H), ((0, 4),), -0.2, 0.2)), 2097.152, 16777.217)
    return {"tokens": tokens, "cotangent": cotangent, "lengths": lengths, "deal": deal, "attn_master": attn_master, "ffin_master": ffin_master, "ffout_master": ffout_master, "gain_master": gain_master, "bias_master": bias_master, "attn_first": attn_first, "ffin_first": ffin_first, "ffout_first": ffout_first, "gain_first": gain_first, "bias_first": bias_first, "attn_second": attn_second, "ffin_second": ffin_second, "ffout_second": ffout_second, "gain_second": gain_second, "bias_second": bias_second}


@jax.custom_vjp
def low(v):
    return lax.optimization_barrier(v.astype(jnp.bfloat16)).astype(jnp.float32)

@jax.custom_vjp
def low_back(v):
    return v

def low_keep(v):
    return (low(v), None)

def low_pass(kept, grad):
    return (grad,)

def back_keep(v):
    return (v, None)

def back_low(kept, grad):
    return (low(grad),)
low.defvjp(low_keep, low_pass)
low_back.defvjp(back_keep, back_low)
norm_eps = 1e-06
far_below = -1e+30
steps_beyond = (12, 16, 23, 32, 46, 64, 91)
first_rate = 0.9
second_rate = 0.95
learning = 0.05
shrink = 0.1
adam_eps = 1e-08
first_fix = 1.0 - 0.9 ** 8
second_fix = 1.0 - 0.95 ** 8

def hi_dot(left, right):
    return jnp.dot(left, right, precision=lax.Precision.HIGHEST, preferred_element_type=jnp.float32)

def bucket_of(relative):
    distance = jnp.abs(relative)
    beyond = 8 + sum(((distance >= threshold).astype(jnp.int32) for threshold in steps_beyond))
    near_part = jnp.where(distance < 8, distance, beyond)
    return (near_part + 16 * (relative > 0).astype(jnp.int32)).astype(jnp.int32)

def places(lengths_row, whole_len):
    starts = (jnp.cumsum(lengths_row) - lengths_row).astype(jnp.int32)
    index_all = jnp.arange(whole_len, dtype=jnp.int32)
    passed = index_all[:, None] >= starts[None, :]
    seg_ids = (lax.optimization_barrier(jnp.sum(passed.astype(jnp.int32), axis=1)) - 1).astype(jnp.int32)
    begins = lax.optimization_barrier(jnp.max(jnp.where(passed, starts[None, :], 0), axis=1)).astype(jnp.int32)
    return (seg_ids, (index_all - begins).astype(jnp.int32))

def rms_scale(values, gain):
    return values * lax.rsqrt(lax.optimization_barrier(jnp.mean(values * values, axis=-1, keepdims=True)) + norm_eps) * gain

def layer(x_val, params, seg_ids, positions):
    attn_w, in_w, out_w, gain_w, bias_w = [low(param) for param in params]
    act_one = low(rms_scale(x_val, gain_w[0]))
    query_all = low(low_back(hi_dot(act_one, attn_w[0])))
    key_all = low(low_back(hi_dot(act_one, attn_w[1])))
    value_all = low(low_back(hi_dot(act_one, attn_w[2])))
    key_heads = key_all.reshape(TOKG, H, HD)
    value_heads = value_all.reshape(TOKG, H, HD)
    block_len = min(512, TOKG)

    def attend_block(block_in):
        query_blk, seg_blk, pos_blk = block_in
        scores = jnp.einsum('qhd,khd->hqk', query_blk, key_heads, precision=lax.Precision.HIGHEST)
        bias_vals = jnp.transpose(bias_w[bucket_of(positions[None, :] - pos_blk[:, None])], (2, 0, 1))
        scores = low_back(scores + bias_vals)
        same_seq = seg_blk[:, None] == seg_ids[None, :]
        prob_vals = jax.nn.softmax(jnp.where(same_seq[None], scores, far_below), axis=-1)
        return jnp.einsum('hqk,khd->qhd', low(prob_vals), value_heads, precision=lax.Precision.HIGHEST)
    attn_mix = lax.map(jax.checkpoint(attend_block), (query_all.reshape(TOKG // block_len, block_len, H, HD), seg_ids.reshape(-1, block_len), positions.reshape(-1, block_len)))
    attn_mix = low(low_back(attn_mix.reshape(TOKG, D)))
    x_mid = x_val + low_back(hi_dot(attn_mix, attn_w[3]))
    act_two = low(rms_scale(x_mid, gain_w[1]))
    gate_pre = low_back(hi_dot(act_two, in_w[0]))
    up_pre = low_back(hi_dot(act_two, in_w[1]))
    hidden = low(jax.nn.gelu(gate_pre, approximate=True) * up_pre)
    return x_mid + low_back(hi_dot(hidden, out_w))

def adam_step(master, first, second, grad, decayed):
    new_first = first_rate * first + (1.0 - first_rate) * grad
    new_second = second_rate * second + (1.0 - second_rate) * grad * grad
    update = new_first / first_fix / (jnp.sqrt(new_second / second_fix) + adam_eps)
    if decayed:
        update = update + shrink * master
    new_master = master - learning * update
    return (new_master, new_first, new_second, new_master.astype(jnp.bfloat16))

def reference(tokens, cotangent, lengths, deal, attn_master, ffin_master, ffout_master, gain_master, bias_master, attn_first, ffin_first, ffout_first, gain_first, bias_first, attn_second, ffin_second, ffout_second, gain_second, bias_second):
    masters = (attn_master, ffin_master, ffout_master, gain_master, bias_master)

    def one_group(grad_sums, inputs):
        group_x, group_cot, group_len, group_deal = inputs
        seg_ids, positions = places(group_len, TOKG)

        def forward(x_val, params):
            return layer(x_val, params, seg_ids, positions)[group_deal]
        out_val, pull = jax.vjp(forward, group_x.astype(jnp.float32), masters)
        grad_x, grad_params = pull(group_cot.astype(jnp.float32))
        grad_sums = jax.tree.map(lambda acc_val, add_val: acc_val + add_val, grad_sums, grad_params)
        return (grad_sums, (out_val.astype(jnp.bfloat16), grad_x.astype(jnp.bfloat16)))
    zero_grads = jax.tree.map(jnp.zeros_like, masters)
    grad_sums, (layer_out, input_grad) = lax.scan(one_group, zero_grads, (tokens, cotangent, lengths, deal))
    attn_res = adam_step(attn_master, attn_first, attn_second, grad_sums[0], True)
    ffin_res = adam_step(ffin_master, ffin_first, ffin_second, grad_sums[1], True)
    ffout_res = adam_step(ffout_master, ffout_first, ffout_second, grad_sums[2], True)
    gain_res = adam_step(gain_master, gain_first, gain_second, grad_sums[3], False)
    bias_res = adam_step(bias_master, bias_first, bias_second, grad_sums[4], False)
    return (layer_out, input_grad, attn_res[0], ffin_res[0], ffout_res[0], gain_res[0] - gain_master, bias_res[0] - bias_master, attn_res[1], ffin_res[1], ffout_res[1], gain_res[1], bias_res[1], attn_res[2][:3], attn_res[2][3], ffin_res[2], ffout_res[2], gain_res[2], bias_res[2], attn_res[3], ffin_res[3], ffout_res[3])
```

```python
import functools
import jax
import jax.numpy as jnp
from jax import lax
from jax.experimental import pallas as pl
from jax.experimental.pallas import tpu as pltpu
from jax.sharding import PartitionSpec as P

norm_eps = 1e-06
far_below = -1e30
steps_beyond = (12, 16, 23, 32, 46, 64, 91)
first_rate = 0.9
second_rate = 0.95
learning = 0.05
shrink = 0.1
adam_eps = 1e-08
first_fix = 1.0 - 0.9**8
second_fix = 1.0 - 0.95**8
f32 = jnp.float32
bf16 = jnp.bfloat16
HEAD = 64
TILE = 128
ROWS = 256


I_M, I_C, I_Z, I_K, I_J, I_ST, I_START = 0, 1, 2, 3, 4, 5, 8


def log2(n):
    return n.bit_length() - 1


def bucket_of(relative):
    distance = jnp.abs(relative)
    beyond = 8 + sum(((distance >= threshold).astype(jnp.int32) for threshold in steps_beyond))
    near_part = jnp.where(distance < 8, distance, beyond)
    return near_part + 16 * (relative > 0).astype(jnp.int32)


def ndot(left, right):
    return lax.dot_general(left, right, (((1,), (1,)), ((), ())), preferred_element_type=f32)


def tdot(left, right):
    return lax.dot_general(left, right, (((0,), (0,)), ((), ())), preferred_element_type=f32)


def mdot(left, right):
    return jnp.dot(left, right, preferred_element_type=f32)


def arrange(vals, me):
    n = len(vals)
    for b in range(log2(n)):
        flip = ((me >> b) & 1) == 1
        vals = [jnp.where(flip, vals[i ^ (1 << b)], vals[i]) for i in range(n)]
    return vals


def join(vals, me):
    vals = arrange(vals, me)
    return vals[0] if len(vals) == 1 else jnp.concatenate(vals, axis=-1)


def chunk_of(ref, me, n):
    width = ref.shape[-1] // n
    got = ref[:, 0:width]
    for i in range(1, n):
        got = jnp.where(me == i, ref[:, i * width : (i + 1) * width], got)
    return got


def whole(shape):
    zeros = (0,) * len(shape)
    return pl.BlockSpec(shape, lambda *_: zeros)


def smem():
    return pl.BlockSpec(memory_space=pltpu.SMEM)


def call(kernel, out_shape, name, in_specs=None, out_specs=None, grid=(), scratch=()):
    kw = {}
    if grid:
        kw["grid"] = grid
    return pl.pallas_call(
        kernel,
        out_shape=out_shape,
        in_specs=in_specs,
        out_specs=out_specs,
        scratch_shapes=list(scratch),
        compiler_params=pltpu.CompilerParams(vmem_limit_bytes=58 * 1024 * 1024),
        name=name,
        **kw,
    )


def tok_col(sc, half, total):
    t = sc[I_ST] + lax.broadcasted_iota(jnp.int32, (half, 1), 0)
    return jnp.where(t >= total, t - total, t)


def match(sc, ids_ref, k, n, half, total):
    tok_rows = total // (2 * n)
    block = sc[I_J] ^ (k * n)
    if ids_ref is None:
        ids = block * tok_rows + lax.broadcasted_iota(jnp.int32, (1, tok_rows), 1)
    else:
        ids = ids_ref[pl.ds(block, 1), :]
    return jnp.where(tok_col(sc, half, total) == ids, 1.0, 0.0).astype(bf16)


def pick_rows(sc_vec, ids, pieces, n, half):
    width = pieces[0].shape[1]

    def kernel(*refs):
        sc = refs[0]
        ids_ref = refs[1] if ids is not None else None
        got = refs[-3:-1]
        acc = mdot(match(sc, ids_ref, 0, n, half, 2 * half), got[0][...])
        acc = acc + mdot(match(sc, ids_ref, 1, n, half, 2 * half), got[1][...])
        refs[-1][...] = acc.astype(bf16)

    extra = [] if ids is None else [ids]
    specs = [smem()] + [whole(a.shape) for a in extra + list(pieces)]
    return call(kernel, jax.ShapeDtypeStruct((half, width), bf16), "pick_rows", specs, whole((half, width)))(
        sc_vec, *extra, *pieces
    )


def put_rows(sc, ids_ref, value, outs, n):
    half = value.shape[0]
    for k in range(2):
        outs[k][...] = tdot(match(sc, ids_ref, k, n, half, 2 * half), value).astype(bf16)


def add_rows(refs, rows):
    got = refs[0][rows, :].astype(f32)
    for r in refs[1:]:
        got = got + r[rows, :].astype(f32)
    return got


def norm_rows(x):
    return lax.rsqrt(jnp.mean(x * x, axis=-1, keepdims=True) + norm_eps)


def seg_of(sc, t):
    got = jnp.zeros(t.shape, jnp.int32)
    for i in range(1, 4):
        got = got + jnp.where(t >= sc[I_START + i], 1, 0)
    return got


def strip_of(vec_row, half):
    wide = jnp.broadcast_to(vec_row, (TILE, 2 * half))
    return pltpu.roll(wide, 0, 1, stride=1, stride_axis=0)


def diagonals(strip, half):
    wide = 2 * half
    acc = strip[0:8, :]
    for a in range(8, TILE, 8):
        acc = acc + pltpu.roll(strip[a : a + 8, :], wide - a, 1)
    row = lax.broadcasted_iota(jnp.int32, (8, 1), 0)
    for b in range(3):
        acc = jnp.where(((row >> b) & 1) == 1, pltpu.roll(acc, wide - (1 << b), 1), acc)
    return jnp.sum(acc, axis=0, keepdims=True)


def head_mask(width, which):
    lane = lax.broadcasted_iota(jnp.int32, (1, width), 1)
    return (lane // HEAD) == which


def segs(sc, half, total):
    t_row = sc[I_ST] + lax.broadcasted_iota(jnp.int32, (1, half), 1)
    t_row = jnp.where(t_row >= total, t_row - total, t_row)
    return seg_of(sc, t_row)


def seg_rows(sc, start, total):
    t = sc[I_ST] + start + lax.broadcasted_iota(jnp.int32, (TILE, 1), 0)
    t = jnp.where(t >= total, t - total, t)
    return seg_of(sc, t)


def attend(sc_vec, xs, gain, w_qkv, vec, total):
    n = len(xs)
    half = xs[0].shape[0]
    width = gain.shape[1]
    mine = w_qkv.shape[2]
    pairs = mine // TILE
    nb = half // TILE

    def kernel(*refs):
        sc = refs[0]
        x_refs = refs[1 : 1 + n]
        gain_ref, w_ref, vec_ref = refs[1 + n : 4 + n]
        a1_ref, q_ref, k_ref, v_ref, o_ref, lse_ref, a_scr, strip = refs[4 + n :]
        g = pl.program_id(0)

        @pl.when(g == 0)
        def _():
            for i in range(half // TILE):
                rows = slice(i * TILE, (i + 1) * TILE)
                x = add_rows(x_refs, rows)
                a1 = (x * norm_rows(x) * gain_ref[...]).astype(bf16)
                a_scr[rows, :] = a1
                a1_ref[rows, :] = a1

        q = mdot(a_scr[...], w_ref[0]).astype(bf16)
        k = mdot(a_scr[...], w_ref[1]).astype(bf16)
        v = mdot(a_scr[...], w_ref[2]).astype(bf16)
        q_ref[...] = q
        k_ref[...] = k
        v_ref[...] = v
        seg_keys = segs(sc, half, total)
        for hh in range(2):
            keep = head_mask(TILE, hh)
            km = jnp.where(keep, k.astype(f32), 0.0).astype(bf16)
            vm = jnp.where(keep, v.astype(f32), 0.0).astype(bf16)
            strip[...] = strip_of(vec_ref[pl.ds(2 * g + hh, 1), :], half)

            def step(i, carry, km=km, vm=vm, keep=keep, hh=hh):
                start = pl.multiple_of(i * TILE, TILE)
                rows = pl.ds(start, TILE)
                s = ndot(q_ref[rows, :], km)
                s = s + strip[:, pl.ds(pl.multiple_of(half - i * TILE, TILE), half)]
                s = jnp.where(seg_rows(sc, start, total) == seg_keys, s, far_below)
                high = jnp.max(s, axis=-1, keepdims=True)
                e = jnp.exp(s - high)
                tot = jnp.sum(e, axis=-1, keepdims=True)
                pb = (e * (1.0 / tot)).astype(bf16)
                o = mdot(pb, vm)
                lse = jnp.broadcast_to(high + jnp.log(tot), (TILE, TILE))
                if hh == 0:
                    o_ref[rows, :] = o.astype(bf16)
                    lse_ref[rows, :] = lse
                else:
                    o_ref[rows, :] = jnp.where(keep, o, o_ref[rows, :].astype(f32)).astype(bf16)
                    lse_ref[rows, :] = jnp.where(keep, lse, lse_ref[rows, :])
                return carry

            lax.fori_loop(0, nb, step, 0)

    def block(dtype):
        return jax.ShapeDtypeStruct((half, mine), dtype)

    pair_spec = pl.BlockSpec((half, TILE), lambda g: (0, g))
    return call(
        kernel,
        (jax.ShapeDtypeStruct((half, width), bf16), block(bf16), block(bf16), block(bf16), block(bf16), block(f32)),
        "attend",
        [smem()] + [whole(x.shape) for x in xs] + [whole(gain.shape), pl.BlockSpec((3, width, TILE), lambda g: (0, 0, g)), whole(vec.shape)],
        [whole((half, width))] + [pair_spec] * 5,
        (pairs,),
        [pltpu.VMEM((half, width), bf16), pltpu.VMEM((TILE, 2 * half), f32)],
    )(sc_vec, *xs, gain, w_qkv, vec)


def ffn_up(sc_vec, xs, os_, w_o, gain, w_in):
    n = len(xs)
    half = xs[0].shape[0]
    width = gain.shape[1]
    hid = w_in.shape[2]

    def kernel(*refs):
        sc = refs[0]
        x_refs = refs[1 : 1 + n]
        o_refs = refs[1 + n : 1 + 2 * n]
        wo_ref, gain_ref, w_ref, x1_ref, a2_ref, g0_ref, g1_ref = refs[1 + 2 * n :]
        o = join([r[...].astype(f32) for r in o_refs], sc[I_M]).astype(bf16)
        x = add_rows(x_refs, slice(None))
        x1 = x + mdot(o, wo_ref[...])
        x1_ref[...] = x1
        a2 = (x1 * norm_rows(x1) * gain_ref[...]).astype(bf16)
        a2_ref[...] = a2
        g0_ref[...] = mdot(a2, w_ref[0])
        g1_ref[...] = mdot(a2, w_ref[1])

    def rows(w):
        return pl.BlockSpec((ROWS, w), lambda i: (i, 0))

    return call(
        kernel,
        (
            jax.ShapeDtypeStruct((half, width), f32),
            jax.ShapeDtypeStruct((half, width), bf16),
            jax.ShapeDtypeStruct((half, hid), f32),
            jax.ShapeDtypeStruct((half, hid), f32),
        ),
        "ffn_up",
        [smem()] + [rows(a.shape[1]) for a in list(xs) + list(os_)] + [whole(w_o.shape), whole(gain.shape), whole(w_in.shape)],
        [rows(width), rows(width), rows(hid), rows(hid)],
        (half // ROWS,),
    )(sc_vec, *xs, *os_, w_o, gain, w_in)


def gelu_parts(u):
    a = 0.7978845608028654
    inner = a * (u + 0.044715 * u * u * u)
    th = jnp.tanh(inner)
    val = 0.5 * u * (1.0 + th)
    slope = 0.5 * (1.0 + th) + 0.5 * u * (1.0 - th * th) * (a * (1.0 + 3.0 * 0.044715 * u * u))
    return val, slope


def ffn_back(sc_vec, dys, g0, g1, w_out, w_in):
    n = len(dys)
    half, hid = g0.shape
    width = w_out.shape[1]

    def kernel(*refs):
        sc = refs[0]
        dy_refs = refs[1 : 1 + n]
        g0_ref, g1_ref, wout_ref, w_ref, dy_ref, hd_ref, dg0_ref, dg1_ref, da2_ref = refs[1 + n :]
        dy = add_rows(dy_refs, slice(None)).astype(bf16)
        dy_ref[...] = dy
        dhd = ndot(dy, wout_ref[...])
        val, slope = gelu_parts(g0_ref[...])
        up = g1_ref[...]
        hd_ref[...] = (val * up).astype(bf16)
        dg0 = (dhd * slope * up).astype(bf16)
        dg1 = (dhd * val).astype(bf16)
        dg0_ref[...] = dg0
        dg1_ref[...] = dg1
        da2_ref[...] = (ndot(dg0, w_ref[0]) + ndot(dg1, w_ref[1])).astype(bf16)

    def rows(w):
        return pl.BlockSpec((ROWS, w), lambda i: (i, 0))

    def out(w):
        return jax.ShapeDtypeStruct((half, w), bf16)

    return call(
        kernel,
        (out(width), out(hid), out(hid), out(hid), out(width)),
        "ffn_back",
        [smem()] + [rows(a.shape[1]) for a in list(dys)] + [rows(hid), rows(hid), whole(w_out.shape), whole(w_in.shape)],
        [rows(width), rows(hid), rows(hid), rows(hid), rows(width)],
        (half // ROWS,),
    )(sc_vec, *dys, g0, g1, w_out, w_in)


def ffn_grads(hd, dg0, dg1, a2, dy, w_out):
    half, hid = hd.shape
    width = w_out.shape[1]
    wide = min(256, hid)
    steps = hid // wide

    def kernel(hd_ref, dg0_ref, dg1_ref, a2_ref, dy_ref, wout_ref, dwout_ref, dwi_ref, y_ref, acc):
        i = pl.program_id(0)
        dwout_ref[...] = tdot(hd_ref[...], dy_ref[...]).astype(bf16)
        dwi_ref[0] = tdot(a2_ref[...], dg0_ref[...]).astype(bf16)
        dwi_ref[1] = tdot(a2_ref[...], dg1_ref[...]).astype(bf16)
        part = mdot(hd_ref[...], wout_ref[...])

        @pl.when(i == 0)
        def _():
            acc[...] = part

        @pl.when(i > 0)
        def _():
            acc[...] = acc[...] + part

        @pl.when(i == steps - 1)
        def _():
            y_ref[...] = acc[...].astype(bf16)

    lanes = pl.BlockSpec((half, wide), lambda i: (0, i))
    return call(
        kernel,
        (
            jax.ShapeDtypeStruct((hid, width), bf16),
            jax.ShapeDtypeStruct((2, width, hid), bf16),
            jax.ShapeDtypeStruct((half, width), bf16),
        ),
        "ffn_grads",
        [lanes, lanes, lanes, whole(a2.shape), whole(dy.shape), pl.BlockSpec((wide, width), lambda i: (i, 0))],
        [pl.BlockSpec((wide, width), lambda i: (i, 0)), pl.BlockSpec((2, width, wide), lambda i: (0, 0, i))]
        + [whole((half, width))],
        (steps,),
        [pltpu.VMEM((half, width), f32)],
    )(hd, dg0, dg1, a2, dy, w_out)


def attend_back(sc_vec, da2s, x1, dy, gain, wo_rows, w_qkv, q, k, v, lse, vec, total):
    n = len(da2s)
    half, width = x1.shape
    mine = q.shape[1]
    pairs = mine // TILE
    nb = half // TILE

    def kernel(*refs):
        sc = refs[0]
        da2_refs = refs[1 : 1 + n]
        x1_ref, dy_ref, gain_ref, wo_ref, w_ref, q_ref, k_ref, v_ref, lse_ref, vec_ref = refs[1 + n : 11 + n]
        dx1_ref, da_ref, dg_ref, dq_ref, dk_ref, dv_ref, da1_ref, dvec_ref = refs[11 + n : 19 + n]
        strip, dstrip, ds_scr, pb_scr, do_scr, dq_scr, dk_scr, dv_scr = refs[19 + n :]
        g = pl.program_id(0)

        @pl.when(g == 0)
        def _():
            dg = jnp.zeros((1, width), f32)
            for i in range(nb):
                rows = slice(i * TILE, (i + 1) * TILE)
                da2 = da2_refs[0][rows, :].astype(f32)
                for r in da2_refs[1:]:
                    da2 = da2 + r[rows, :].astype(f32)
                x = x1_ref[rows, :]
                r2 = norm_rows(x)
                e2 = da2 * gain_ref[...]
                dx1 = dy_ref[rows, :].astype(f32) + r2 * e2 - x * (r2 * r2 * r2 * jnp.mean(e2 * x, axis=-1, keepdims=True))
                dg = dg + jnp.sum(da2 * x * r2, axis=0, keepdims=True)
                dx1_ref[rows, :] = dx1
                da_ref[rows, :] = dx1.astype(bf16)
            dg_ref[...] = dg

        do_scr[...] = ndot(da_ref[...], wo_ref[...]).astype(bf16)
        seg_keys = segs(sc, half, total)
        kk = k_ref[...].astype(f32)
        vv = v_ref[...].astype(f32)
        dq_tot = None
        for hh in range(2):
            keep = head_mask(TILE, hh)
            km = jnp.where(keep, kk, 0.0).astype(bf16)
            vm = jnp.where(keep, vv, 0.0).astype(bf16)
            strip[...] = strip_of(vec_ref[pl.ds(2 * g + hh, 1), :], half)
            dstrip[...] = jnp.zeros_like(dstrip)

            def step(i, carry, km=km, vm=vm, hh=hh):
                start = pl.multiple_of(i * TILE, TILE)
                rows = pl.ds(start, TILE)
                lanes = pl.ds(pl.multiple_of(half - i * TILE, TILE), half)
                s = ndot(q_ref[rows, :], km) + strip[:, lanes]
                same = seg_rows(sc, start, total) == seg_keys
                lse_col = lse_ref[rows, :][:, hh * HEAD : hh * HEAD + 1]
                p = jnp.exp(jnp.where(same, s - lse_col, far_below))
                dp = ndot(do_scr[rows, :], vm)
                delta = jnp.sum(p * dp, axis=-1, keepdims=True)
                ds = (p * (dp - delta)).astype(bf16)
                pb_scr[rows, :] = p.astype(bf16)
                ds_scr[rows, :] = ds
                dstrip[:, lanes] = dstrip[:, lanes] + ds.astype(f32)
                return carry

            lax.fori_loop(0, nb, step, 0)
            qm = jnp.where(keep, q_ref[...].astype(f32), 0.0).astype(bf16)
            dom = jnp.where(keep, do_scr[...].astype(f32), 0.0).astype(bf16)
            dqh = mdot(ds_scr[...], km)
            dkh = tdot(ds_scr[...], qm)
            dvh = tdot(pb_scr[...], dom)
            if hh == 0:
                dq_tot, dk_tot, dv_tot = dqh, dkh, dvh
            else:
                dq_tot, dk_tot, dv_tot = dq_tot + dqh, dk_tot + dkh, dv_tot + dvh
            dvec_ref[0, hh : hh + 1, :] = diagonals(dstrip, half)
        dq_ref[...] = dq_tot.astype(bf16)
        dk_ref[...] = dk_tot.astype(bf16)
        dv_ref[...] = dv_tot.astype(bf16)
        dq_scr[g] = dq_ref[...]
        dk_scr[g] = dk_ref[...]
        dv_scr[g] = dv_ref[...]

        @pl.when(g == pairs - 1)
        def _():
            acc = None
            for i in range(pairs):
                lanes = slice(i * TILE, (i + 1) * TILE)
                for mat, scr in enumerate((dq_scr, dk_scr, dv_scr)):
                    part = ndot(scr[i], w_ref[mat, :, lanes])
                    acc = part if acc is None else acc + part
            da1_ref[...] = acc.astype(bf16)

    pair_spec = pl.BlockSpec((half, TILE), lambda g: (0, g))
    big = jax.ShapeDtypeStruct((half, width), bf16)
    head = jax.ShapeDtypeStruct((half, mine), bf16)
    return call(
        kernel,
        (
            jax.ShapeDtypeStruct((half, width), f32),
            big,
            jax.ShapeDtypeStruct((1, width), f32),
            head,
            head,
            head,
            big,
            jax.ShapeDtypeStruct((pairs, 8, 2 * half), f32),
        ),
        "attend_back",
        [smem()]
        + [whole(a.shape) for a in da2s]
        + [whole(x1.shape), whole(dy.shape), whole(gain.shape), pl.BlockSpec((TILE, width), lambda g: (g, 0)), whole(w_qkv.shape)]
        + [pair_spec] * 4
        + [whole(vec.shape)],
        [whole((half, width)), whole((half, width)), whole((1, width)), pair_spec, pair_spec, pair_spec, whole((half, width))]
        + [pl.BlockSpec((1, 8, 2 * half), lambda g: (g, 0, 0))],
        (pairs,),
        [
            pltpu.VMEM((TILE, 2 * half), f32),
            pltpu.VMEM((TILE, 2 * half), f32),
            pltpu.VMEM((half, half), bf16),
            pltpu.VMEM((half, half), bf16),
            pltpu.VMEM((half, TILE), bf16),
            pltpu.VMEM((pairs, half, TILE), bf16),
            pltpu.VMEM((pairs, half, TILE), bf16),
            pltpu.VMEM((pairs, half, TILE), bf16),
        ],
    )(sc_vec, *da2s, x1, dy, gain, wo_rows, w_qkv, q, k, v, lse, vec)


def wo_grads(sc_vec, o, da):
    mine = o.shape[1]
    width = da.shape[1]

    def kernel(sc, o_ref, da_ref, keep_ref, send_ref):
        got = tdot(o_ref[...], da_ref[...])
        lo, hi = got[:, : width // 2], got[:, width // 2 :]
        first = sc[I_C] == 0
        keep_ref[...] = jnp.where(first, lo, hi).astype(bf16)
        send_ref[...] = jnp.where(first, hi, lo).astype(bf16)

    out = jax.ShapeDtypeStruct((mine, width // 2), bf16)
    return call(
        kernel, (out, out), "wo_grads", [smem(), whole(o.shape), whole(da.shape)], [whole(out.shape)] * 2
    )(sc_vec, o, da)


def qkv_grads(a1, dq, dk, dv):
    half, width = a1.shape
    mine = dq.shape[1]

    def kernel(a_ref, q_ref, k_ref, v_ref, out_ref):
        for i, r in enumerate((q_ref, k_ref, v_ref)):
            out_ref[i] = tdot(a_ref[...], r[...]).astype(bf16)

    return call(
        kernel,
        jax.ShapeDtypeStruct((3, width, mine), bf16),
        "qkv_grads",
        [whole(a.shape) for a in (a1, dq, dk, dv)],
        whole((3, width, mine)),
    )(a1, dq, dk, dv)


def send_y(sc_vec, deal, ys, x1, n):
    half, width = x1.shape
    m = len(ys)

    def kernel(*refs):
        sc, deal_ref = refs[:2]
        y = refs[2 + m][...] + add_rows(refs[2 : 2 + m], slice(None))
        put_rows(sc, deal_ref, y.astype(bf16), refs[3 + m :], n)

    out = jax.ShapeDtypeStruct((half // n, width), bf16)
    return call(
        kernel,
        (out,) * 2,
        "send_y",
        [smem(), whole(deal.shape)] + [whole(y.shape) for y in ys] + [whole(x1.shape)],
        [whole(out.shape)] * 2,
    )(sc_vec, deal, *ys, x1)


def send_dx(sc_vec, da1s, xs, dx1, gain, n):
    half, width = dx1.shape
    m = len(da1s)

    def kernel(*refs):
        sc = refs[0]
        da1_refs = refs[1 : 1 + m]
        x_refs = refs[1 + m : 1 + 2 * m]
        dx1_ref, gain_ref, dg_ref = refs[1 + 2 * m : 4 + 2 * m]
        outs = refs[4 + 2 * m : -1]
        dx_scr = refs[-1]
        dg = jnp.zeros((1, width), f32)
        for i in range(half // TILE):
            rows = slice(i * TILE, (i + 1) * TILE)
            da1 = add_rows(da1_refs, rows)
            x = add_rows(x_refs, rows)
            r1 = norm_rows(x)
            e1 = da1 * gain_ref[...]
            dx = dx1_ref[rows, :] + r1 * e1 - x * (r1 * r1 * r1 * jnp.mean(e1 * x, axis=-1, keepdims=True))
            dg = dg + jnp.sum(da1 * x * r1, axis=0, keepdims=True)
            dx_scr[rows, :] = dx.astype(bf16)
        dg_ref[...] = dg
        put_rows(sc, None, dx_scr[...], outs, n)

    out = jax.ShapeDtypeStruct((half // n, width), bf16)
    return call(
        kernel,
        (jax.ShapeDtypeStruct((1, width), f32),) + (out,) * 2,
        "send_dx",
        [smem()] + [whole(a.shape) for a in list(da1s) + list(xs)] + [whole(dx1.shape), whole(gain.shape)],
        [whole((1, width))] + [whole(out.shape)] * 2,
        (),
        [pltpu.VMEM((half, width), bf16)],
    )(sc_vec, *da1s, *xs, dx1, gain)


def blocks_of(shapes, parts):
    got, at = [], 0
    for a, (nm, rs, w) in enumerate(shapes):
        for mat in range(nm):
            for b in range(w // TILE):
                got.append((a, mat, b, rs // parts, at))
                at += rs // parts
    return got, at


def prepare(sc_vec, arrays, places, shapes, parts, tail):
    plan, size = blocks_of(shapes, parts)
    extra = 0 if tail is None else tail.shape[0]
    n = len(arrays)

    def kernel(*refs):
        sc = refs[0]
        src = refs[1 : 1 + n]
        own_ref, part_ref = refs[-2:]
        mine = sc[I_K] % parts
        for a, mat, b, pr, at in plan:
            row, lane = places(a, mat, b, sc[I_C])
            for i in range(parts):
                rows = pl.ds(row + i * pr, pr)
                own_ref[i, at : at + pr, :] = src[a][mat, rows, pl.ds(pl.multiple_of(lane, TILE), TILE)].astype(bf16)
        part_ref[0, :size, :] = own_ref[mine]
        if extra:
            part_ref[0, size:, :] = refs[1 + n][...]

    tails = [] if tail is None else [tail]
    outs = (jax.ShapeDtypeStruct((parts, size, TILE), bf16), jax.ShapeDtypeStruct((1, size + extra, TILE), bf16))
    return call(
        kernel, outs, "prepare", [smem()] + [whole(a.shape) for a in list(arrays) + tails], [whole(o.shape) for o in outs]
    )(sc_vec, *arrays, *tails)


def unpack(sc_vec, own, got, shapes, shards, parts):
    plan, _ = blocks_of(shapes, parts)

    def kernel(*refs):
        sc, own_ref = refs[:2]
        pieces = refs[2 : 2 + len(got)]
        outs = refs[2 + len(got) :]

        def put(src, at_src, quarter, part):
            for a, mat, b, pr, at in plan:
                row = pl.multiple_of(quarter * shapes[a][1] + part * pr, 16)
                outs[a][mat, pl.ds(row, pr), b * TILE : (b + 1) * TILE] = src[at_src, at : at + pr, :]

        for part in range(parts):
            put(own_ref, part, sc[I_Z], part)
        for ref, (keys, off, _) in zip(pieces, got):
            for i, k in enumerate(keys):
                put(ref, i, sc[I_Z] ^ k, (sc[I_K] % parts) ^ off)

    outs = tuple(jax.ShapeDtypeStruct((nm, shards * rs, w), bf16) for nm, rs, w in shapes)
    return call(
        kernel,
        outs,
        "unpack",
        [smem(), whole(own.shape)] + [whole(a.shape) for _, _, a in got],
        [whole(o.shape) for o in outs],
    )(sc_vec, own, *[a for _, _, a in got])


def split_up(sc_vec, grads, shapes, shards, parts, sets):
    plan, size = blocks_of(shapes, parts)
    n = len(grads)

    def kernel(*refs):
        sc = refs[0]
        src = refs[1 : 1 + n]
        for out, keys in zip(refs[1 + n :], sets):
            for i, (off, k) in enumerate(keys):
                part = (sc[I_K] % parts) ^ off
                for a, mat, b, pr, at in plan:
                    row = pl.multiple_of((sc[I_Z] ^ k) * shapes[a][1] + part * pr, 16)
                    out[i, at : at + pr, :] = src[a][mat, pl.ds(row, pr), b * TILE : (b + 1) * TILE]

    outs = tuple(jax.ShapeDtypeStruct((len(keys), size, TILE), bf16) for keys in sets)
    return call(
        kernel, outs, "split_up", [smem()] + [whole(g.shape) for g in grads], [whole(o.shape) for o in outs]
    )(sc_vec, *grads)


def adam_math(w, m, v, g, decayed):
    new_m = first_rate * m + (1.0 - first_rate) * g
    new_v = second_rate * v + (1.0 - second_rate) * g * g
    update = new_m / first_fix / (jnp.sqrt(new_v / second_fix) + adam_eps)
    if decayed:
        update = update + shrink * w
    new_w = w - learning * update
    return new_w, new_m, new_v


def adam(sc_vec, mine, other, shapes, parts, params, places, seconds, name):
    plan, size = blocks_of(shapes, parts)
    n = len(params)

    def kernel(*refs):
        sc = refs[0]
        mine_ref, other_ref = refs[1:3]
        ins = [refs[3 + 3 * a : 6 + 3 * a] for a in range(n)]
        at_out = 3 + 3 * n
        outs = []
        for a in range(n):
            count = 3 + len(seconds[a])
            outs.append(refs[at_out : at_out + count])
            at_out += count
        off = pl.program_id(0) ^ (sc[I_K] % parts)
        first_core = sc[I_C] == 0
        for a, mat, b, pr, at in plan:
            own = mine_ref[off, at : at + pr, :].astype(f32)
            oth = other_ref[off, at : at + pr, :].astype(f32)
            for core in range(2):
                g = jnp.where(first_core, own, oth) if core == 0 else jnp.where(first_core, oth, own)
                lead, lane = places(a, mat, b, core)
                lanes = slice(lane, lane + TILE)
                w_ref, m_ref, v_ref = ins[a]
                nw, nm_, nv = adam_math(w_ref[lead][:, lanes], m_ref[lead][:, lanes], v_ref[lead][:, lanes], g, True)
                nw_ref, nm_ref, cp_ref = outs[a][:3]
                nw_ref[lead + (slice(None), lanes)] = nw
                nm_ref[lead + (slice(None), lanes)] = nm_
                cp_ref[lead + (slice(None), lanes)] = nw.astype(bf16)
                at_v = lead[0]
                for which, cnt in enumerate(seconds[a]):
                    if at_v < cnt:
                        outs[a][3 + which][(at_v,) + lead[1:] + (slice(None), lanes)] = nv
                        break
                    at_v -= cnt

    in_specs = [smem(), whole(mine.shape), whole(other.shape)]
    out_specs, out_shape = [], []
    for a, (master, _, _) in enumerate(params):
        lead = master.shape[:-2]
        rows, w = master.shape[-2:]
        if len(lead) == 1:
            rows //= parts

            def spec(count, rows=rows, w=w):
                return pl.BlockSpec((count, rows, w), lambda i: (0, i, 0))

        else:

            def spec(count, rows=rows, w=w):
                return pl.BlockSpec((count, 1, rows, w), lambda i: (0, i, 0, 0))

        in_specs += [spec(lead[0])] * 3
        for dtype in (f32, f32, bf16):
            out_specs.append(spec(lead[0]))
            out_shape.append(jax.ShapeDtypeStruct(master.shape, dtype))
        for cnt in seconds[a]:
            out_specs.append(spec(cnt))
            out_shape.append(jax.ShapeDtypeStruct((cnt,) + master.shape[1:], f32))
    return call(kernel, tuple(out_shape), name, in_specs, out_specs, (parts,))(
        sc_vec, mine, other, *[x for trio in params for x in trio]
    )


def parts_for(rs, plane):
    parts = plane
    while parts > 1 and (rs % parts or (rs // parts) % 16):
        parts //= 2
    return parts


def body(
    tokens,
    cotangent,
    lengths,
    deal,
    attn_master,
    ffin_master,
    ffout_master,
    gain_master,
    bias_master,
    attn_first,
    ffin_first,
    ffout_first,
    gain_first,
    bias_first,
    attn_second,
    ffin_second,
    ffout_second,
    gain_second,
    bias_second,
):
    S = lax.axis_size("shard")
    reps = lax.axis_size("rep")
    plane = reps // 2
    Q = S // 4
    M = 2 * Q
    tok_rows, D = tokens.shape[1:]
    T = tok_rows * S
    half = T // 2
    H = bias_master.shape[1]
    NBS = bias_master.shape[0]
    NB = NBS * S
    Ds = attn_master.shape[1]
    FF = ffin_master.shape[2]
    Dm = D // M
    Dp = -(-Dm // TILE) * TILE
    FFm = FF // M
    zbits = log2(S)

    z = lax.axis_index("shard")
    rep = lax.axis_index("rep")
    c = rep % 2
    kap = rep // 2
    job = z // Q
    q_at = z % Q
    p = job // 2
    hf = job % 2
    m = c * Q + q_at
    j = hf * M + m

    def move(x, to):
        perm = [(r * S + s, (lambda a: a[0] * S + a[1])(to(r, s))) for r in range(reps) for s in range(S)]
        return lax.ppermute(x, ("rep", "shard"), perm)

    def over_shard(x, bit):
        return move(x, lambda r, s: (r, s ^ bit))

    def over_plane(x, bit):
        return move(x, lambda r, s: (r ^ (2 * bit), s))

    def over_core(x):
        return move(x, lambda r, s: (r ^ 1, s))

    def deliver(x, k):
        def to(r, s):
            mm = s % M
            return (2 * (r // 2) + mm // Q, (2 * (r % 2) + ((s // M) ^ k)) * Q + mm % Q)

        return move(x, to)

    def give_back(x, k):
        def to(r, s):
            jb = s // Q
            return (2 * (r // 2) + jb // 2, ((jb % 2) ^ k) * M + (r % 2) * Q + s % Q)

        return move(x, to)

    def among(x, bit):
        def to(r, s):
            mm = ((r % 2) * Q + s % Q) ^ bit
            return (2 * (r // 2) + mm // Q, (s // Q) * Q + mm % Q)

        return move(x, to)

    def members(x):
        return [x] + [among(x, i) for i in range(1, M)]

    ints = jnp.concatenate([lengths[0], deal[0]])
    ints_other = over_core(ints)
    ints = jnp.where(p == c, ints, ints_other)
    lens, deal_p = ints[:4], ints[4:].reshape(S, tok_rows)
    order = jnp.arange(4, dtype=jnp.int32)
    starts = jnp.sum(jnp.where(order[None, :] < order[:, None], lens[None, :], 0), axis=1)
    st = jnp.sum(jnp.where(lens == half, starts, 0)) + hf * half
    st = jnp.where(st >= T, st - T, st)
    lane16 = jnp.arange(16, dtype=jnp.int32)
    sc = jnp.sum(jnp.where(lane16[:, None] == order[None, :] + I_START, starts[None, :], 0), axis=1)
    for at, val in ((I_M, m), (I_C, c), (I_Z, z), (I_K, kap), (I_J, j), (I_ST, st)):
        sc = jnp.where(lane16 == at, val.astype(jnp.int32), sc)

    x_pieces = [deliver(tokens[0], k) for k in range(2)]

    parts = min(parts_for(Ds, plane), parts_for(FF // (2 * S), plane))
    nbits = log2(parts)
    Fr = FF // (2 * S)
    a_shapes = [(4, Ds, D // 2)]
    f_shapes = [(2, Ds, FF // 2), (1, Fr, D)]

    def a_place(a, mat, b, core):
        return 0, core * (D // 2) + b * TILE

    def f_place(a, mat, b, core):
        if a == 0:
            return 0, (b * TILE // Fr) * 2 * Fr + core * Fr + b * TILE % Fr
        return core * Fr, b * TILE

    small = jnp.concatenate([gain_master.reshape(-1), bias_master.reshape(-1)]).astype(bf16)
    n_small = small.shape[0]
    small = jnp.pad(small, (0, -n_small % (16 * TILE))).reshape(-1, TILE)

    def gather(own, part, shapes, turn):
        sets = []
        cur, keys = part, [0]
        for b in reversed(range(zbits)):
            recv = over_shard(cur, 1 << b)
            sets.append(([k ^ (1 << b) for k in keys], recv))
            keys = keys + sets[-1][0]
            if b:
                cur = jnp.concatenate([cur, recv])
        got = []
        for i, (ks, arr) in enumerate(sets):
            bits = list(range(nbits))
            if (i + turn) % 2:
                bits.reverse()
            here = {0: arr}
            for b in bits:
                here.update({off ^ (1 << b): over_plane(a, 1 << b) for off, a in here.items()})
            got += [(ks, off, a) for off, a in here.items()]
        return unpack(sc, own, got, shapes, S, parts), sets

    own_a, part_a = prepare(sc, [attn_master], a_place, a_shapes, parts, small)
    (w_attn,), a_sets = gather(own_a, part_a, a_shapes, 0)
    own_f, part_f = prepare(sc, [ffin_master, ffout_master[None]], f_place, f_shapes, parts, None)
    (w_in, w_out), _ = gather(own_f, part_f, f_shapes, 1)
    w_out = w_out[0]
    dy_pieces = [deliver(cotangent[0], k) for k in range(2)]

    tail_rows = small.shape[0]
    tails = {0: small}
    for ks, arr in a_sets:
        for i, k in enumerate(ks):
            tails[k] = arr[i, -tail_rows:, :]
    small_all = jnp.stack([tails[k].reshape(-1)[:n_small] for k in range(S)])
    pickz = (jnp.arange(S)[:, None] ^ jnp.arange(S)[None, :]) == z
    small_all = jnp.dot(pickz.astype(bf16), small_all, preferred_element_type=f32)
    gains = jnp.transpose(small_all[:, : 2 * Ds].reshape(S, 2, Ds), (1, 0, 2)).reshape(2, 1, D)
    table = small_all[:, 2 * Ds :].reshape(NB, H)
    buckets = bucket_of(jnp.arange(2 * half, dtype=jnp.int32) - half)
    hot = (buckets[:, None] == jnp.arange(NB, dtype=jnp.int32)[None, :]).astype(f32)
    heads_here = Dp // HEAD
    head_at = m * (H // M) + jnp.arange(heads_here)
    mine_hot = (jnp.arange(H)[:, None] == head_at[None, :]) & (jnp.arange(heads_here) < H // M)[None, :]
    table_m = jnp.dot(table.astype(bf16), mine_hot.astype(bf16), preferred_element_type=f32)
    vec = lax.dot_general(table_m.astype(bf16), hot.astype(bf16), (((0,), (1,)), ((), ())), preferred_element_type=f32)

    def member_cols(w, n_cols):
        if Q == 1:
            return w
        return lax.dynamic_slice_in_dim(w, q_at * n_cols, n_cols, w.ndim - 1)

    def pad_cols(w):
        return w if Dp == Dm else jnp.pad(w, [(0, 0)] * (w.ndim - 1) + [(0, Dp - Dm)])

    w_qkv = pad_cols(member_cols(w_attn[:3], Dm))
    wo_half = w_attn[3]
    wo_other = over_core(wo_half)
    w_o = jnp.concatenate(arrange([wo_half, wo_other], c), axis=1)
    wo_rows = lax.dynamic_slice_in_dim(w_o, m * Dm, Dm, 0)
    if Dp != Dm:
        wo_rows = jnp.pad(wo_rows, ((0, Dp - Dm), (0, 0)))
    w_in_m = member_cols(w_in, FFm)
    w_out_m = w_out if Q == 1 else lax.dynamic_slice_in_dim(w_out, q_at * FFm, FFm, 0)

    xs = members(pick_rows(sc, None, x_pieces, M, half))
    a1, qh, kh, vh, oh, lse = attend(sc, xs, gains[0], w_qkv, vec, T)
    o_mine = oh[:, :Dm]
    os_ = members(o_mine)
    x1, a2, g0, g1 = ffn_up(sc, xs, os_, w_o, gains[1], w_in_m)

    dys = members(pick_rows(sc, deal_p, dy_pieces, M, half))
    dy, hd, dg0, dg1, da2_part = ffn_back(sc, dys, g0, g1, w_out_m, w_in_m)
    da2s = members(da2_part)
    d_out, d_in, y_part = ffn_grads(hd, dg0, dg1, a2, dy, w_out_m)
    y_back = [give_back(a, k) for k, a in enumerate(send_y(sc, deal_p, members(y_part), x1, M))]
    dx1, da, dgain2, dq, dk, dv, da1_part, dvec = attend_back(
        sc, da2s, x1, dy, gains[1], wo_rows, w_qkv, qh, kh, vh, lse, vec, T
    )
    da1s = members(da1_part)
    wo_keep, wo_send = wo_grads(sc, o_mine, da)
    wo_got = over_core(wo_send)
    d_qkv = qkv_grads(a1, dq, dk, dv)
    dx_out = send_dx(sc, da1s, xs, dx1, gains[0], M)
    dgain1 = dx_out[0]
    x_back = [give_back(a, k) for k, a in enumerate(dx_out[1:])]

    def finish(pieces):
        return (pieces[0].astype(f32) + pieces[1].astype(f32)).astype(bf16)[None]

    layer_out = finish(y_back)
    input_grad = finish(x_back)

    def half_cols(g, axis, count, n):
        if Q == 1:
            return g
        shape = list(g.shape)
        shape[axis] = count
        return lax.dynamic_update_slice_in_dim(jnp.zeros(shape, g.dtype), g, q_at * n, axis)

    def reduce_all(grads, shapes):
        groups = []
        sets = []
        for first_k in (0, S // 2):
            ks = list(range(first_k, first_k + S // 2))
            bits = list(range(nbits))
            if first_k:
                bits.reverse()
            groups.append((ks, bits))
            for side in range(2 if nbits else 1):
                offs = [off for off in range(parts) if not nbits or (off >> bits[0]) & 1 == side]
                for b in bits[1:]:
                    offs = sorted(offs, key=lambda o, b=b: (o >> b) & 1)
                offs = sorted(offs, key=lambda o: tuple((o >> b) & 1 for b in bits[1:]))
                sets.append([(off, k) for off in offs for k in ks])
        arrays = list(split_up(sc, grads, shapes, S, parts, sets))
        final = {}
        for ks, bits in groups:
            if bits:
                keep, send = arrays[:2]
                arrays = arrays[2:]
                total = keep.astype(f32) + over_plane(send, 1 << bits[0]).astype(f32)
                for b in bits[1:]:
                    n = total.shape[0] // 2
                    total = total[:n] + over_plane(total[n:].astype(bf16), 1 << b).astype(f32)
            else:
                total = arrays.pop(0).astype(f32)
            for i, k in enumerate(ks):
                final[k] = total[i]
        for b in range(zbits):
            bit = 1 << b
            stay = [k for k in sorted(final) if not k & bit]
            recv = over_shard(jnp.stack([final[k ^ bit] for k in stay]).astype(bf16), bit)
            final = {k: final[k] + recv[i].astype(f32) for i, k in enumerate(stay)}
        total = final[0]
        extra = parts
        while extra < plane:
            total = total + over_plane(total.astype(bf16), extra).astype(f32)
            extra *= 2
        mine = total.astype(bf16)[None]
        for b in range(nbits):
            mine = jnp.concatenate([mine, over_plane(mine, 1 << b)])
        return mine, over_core(mine)

    d_out_h = half_cols(d_out, 0, FF // 2, FFm)
    d_in_h = half_cols(d_in, 2, FF // 2, FFm)
    d_qkv_h = half_cols(d_qkv[:, :, :Dm], 2, D // 2, Dm)
    if Q == 1:
        d_wo_h = jnp.concatenate(arrange([wo_keep, wo_got], c), axis=0)
    else:
        d_wo_h = jnp.zeros((D, D // 2), bf16)
        d_wo_h = lax.dynamic_update_slice_in_dim(d_wo_h, wo_keep, m * Dm, 0)
        d_wo_h = lax.dynamic_update_slice_in_dim(d_wo_h, wo_got, (m ^ Q) * Dm, 0)
    f_mine, f_other = reduce_all([d_in_h, d_out_h[None]], f_shapes)
    a_mine, a_other = reduce_all([jnp.concatenate([d_qkv_h, d_wo_h[None]])], a_shapes)

    d_table = lax.dot_general(
        dvec[:, :2, :].reshape(heads_here, 2 * half), hot, (((1,), (0,)), ((), ())), precision=lax.Precision.HIGHEST
    )
    d_table = lax.dot_general(
        d_table, mine_hot.astype(f32), (((0,), (1,)), ((), ())), precision=lax.Precision.HIGHEST
    )
    cols_mine = (jnp.arange(D) // Dm) == m
    d_gains = jnp.where(cols_mine[None, :], jnp.concatenate([dgain1, dgain2]), 0.0)
    little = jnp.concatenate([d_gains.reshape(-1), d_table.reshape(-1)])
    little = jnp.pad(little, (0, -little.shape[0] % 1024)).reshape(-1, 128)
    little = little + over_core(little)
    for b in range(log2(plane)):
        little = little + over_plane(little, 1 << b)
    for b in range(zbits):
        little = little + over_shard(little, 1 << b)
    little = little.reshape(-1)
    g_gain = lax.dynamic_slice_in_dim(little[: 2 * D].reshape(2, D), z * Ds, Ds, 1)
    g_bias = lax.dynamic_slice_in_dim(little[2 * D : 2 * D + NB * H].reshape(NB, H), z * NBS, NBS, 0)

    def attn_at(a, mat, b, core):
        return (mat,), core * (D // 2) + b * TILE

    def ffn_at(a, mat, b, core):
        if a == 0:
            return (mat,), (b * TILE // Fr) * 2 * Fr + core * Fr + b * TILE % Fr
        return (core, 0), b * TILE

    view = (2, parts, Fr // parts, D)
    ffn_params = [
        (ffin_master, ffin_first, ffin_second),
        (ffout_master.reshape(view), ffout_first.reshape(view), ffout_second.reshape(view)),
    ]
    ffin_new, ffin_m, ffin_c, ffin_v, ffout_new, ffout_m, ffout_c, ffout_v = adam(
        sc, f_mine, f_other, f_shapes, parts, ffn_params, ffn_at, [(2,), (2,)], "adam_ffn"
    )
    ffout_new, ffout_m, ffout_c, ffout_v = [a.reshape(2 * Fr, D) for a in (ffout_new, ffout_m, ffout_c, ffout_v)]
    attn_new, attn_m, attn_c, attn_v, wo_v = adam(
        sc, a_mine, a_other, a_shapes, parts, [(attn_master, attn_first, attn_second)], attn_at, [(3, 1)], "adam_attn"
    )
    wo_v = wo_v[0]
    gain_new, gain_m, gain_v = adam_math(gain_master, gain_first, gain_second, g_gain, False)
    bias_new, bias_m, bias_v = adam_math(bias_master, bias_first, bias_second, g_bias, False)
    return (
        layer_out,
        input_grad,
        attn_new,
        ffin_new,
        ffout_new,
        gain_new - gain_master,
        bias_new - bias_master,
        attn_m,
        ffin_m,
        ffout_m,
        gain_m,
        bias_m,
        attn_v,
        wo_v,
        ffin_v,
        ffout_v,
        gain_v,
        bias_v,
        attn_c,
        ffin_c,
        ffout_c,
    )
def solution(mesh):
    in_specs = (
        P("rep", "shard", None),
        P("rep", "shard", None),
        P("rep", None),
        P("rep", None),
        P(None, "shard", None),
        P(None, "shard", None),
        P("shard", None),
        P(None, "shard"),
        P("shard", None),
        P(None, "shard", None),
        P(None, "shard", None),
        P("shard", None),
        P(None, "shard"),
        P("shard", None),
        P(None, "shard", None),
        P(None, "shard", None),
        P("shard", None),
        P(None, "shard"),
        P("shard", None),
    )
    out_specs = (
        P("rep", "shard", None),
        P("rep", "shard", None),
        P(None, "shard", None),
        P(None, "shard", None),
        P("shard", None),
        P(None, "shard"),
        P("shard", None),
        P(None, "shard", None),
        P(None, "shard", None),
        P("shard", None),
        P(None, "shard"),
        P("shard", None),
        P(None, "shard", None),
        P("shard", None),
        P(None, "shard", None),
        P("shard", None),
        P(None, "shard"),
        P("shard", None),
        P(None, "shard", None),
        P(None, "shard", None),
        P("shard", None),
    )
    return jax.shard_map(body, mesh=mesh, in_specs=in_specs, out_specs=out_specs, check_vma=False)
```
